32 devices in a mesh: harm: 2 (over y), sx: 4 (over z), sy: 4 (over x, core).
Axes of the slice: x: 2, y: 2, z: 4, core: 2. Of those that a mesh axis runs over, the one named last changes fastest.
Arguments:
- potential_start: float32 [32, 16, 256, 512], P('harm', None, 'sx', 'sy'), may hold values from -6 to 6
- material: int32 [16, 256, 512], P(None, 'sx', 'sy'), may hold values from 0 to 2
- coil_amps: int32 [32], P('harm'), may hold values from -4 to 4
- nu_low: float32 [3], replicated, may hold values from 0.2 to 1
- nu_rise: float32 [3], replicated, may hold values from 0.5 to 2
- conductivity: float32 [3], replicated, may hold values from 0.5 to 4
Outputs:
- potential: float32 [32, 16, 256, 512], P('harm', None, 'sx', 'sy')
- heat_density: float32 [16, 256, 512], P('harm', 'sx', 'sy')
The draws below stay inside these ranges and needn't reach their ends.
All inputs are finite; a program needn't handle non-finite values.
Results may differ from the reference program's by a relative error of at most 0.0003.
Values sent between devices are 32-bit elements; how exact they have to be, the bound alone decides.
No kernel may reach another device: no remote copies, remote signals or barrier semaphores. Data moves between devices by JAX's collectives and lax.ppermute only.
A program may use at most 256 MiB of HBM per device.

```python
import math
import jax
import jax.numpy as jnp
from jax import lax

COEFS = 32
NT = 128
NZ = 16
ITERS = 3
NX = 256
NY = 512


def place_ends(values, key, smallest, largest):
    dims = values.shape
    index_at = [jax.random.randint(jax.random.fold_in(key, axis), (), 0, dims[axis]) for axis in range(len(dims))]
    values = values.at[tuple(index_at)].set(smallest)
    longest = dims.index(max(dims))
    index_at[longest] = (index_at[longest] + 1) % dims[longest]
    return values.at[tuple(index_at)].set(largest)


def shard_levels(stream_key, shape, split, least, high):
    def one(axis_at, blocks):
        draws = jax.random.uniform(jax.random.fold_in(jax.random.fold_in(stream_key, 6), axis_at), (blocks,), jnp.float32, least / len(split), high / len(split))
        return jnp.repeat(jnp.exp(draws), shape[axis_at] // blocks).reshape((-1,) + (1,) * (len(shape) - axis_at - 1))

    loudness = one(*split[0])
    for cut in split[1:]:
        loudness = loudness * one(*cut)
    return loudness


def normal_values(stream_key, shape, spread, bound, cuts=(), held_as=jnp.bfloat16):
    gain = shard_levels(stream_key, shape, cuts, -0.22, 0.18) if cuts else 1.0
    drawn = jax.random.normal(stream_key, shape, jnp.float32) * spread * gain
    return jnp.minimum(jnp.maximum(drawn, -bound), bound).astype(held_as)


def setup_inputs(seed: int = 0) -> dict:
    key_of = jax.random.split(jax.random.key(seed), 7)
    potential_start = normal_values(key_of[0], (COEFS, NZ, NX, NY), 1.0, 6.0, ((0, 2), (2, 4), (3, 4)), jnp.float32)
    material = place_ends(jax.random.randint(key_of[1], (NZ, NX, NY), 0, 3), jax.random.fold_in(key_of[1], 1), 0, 2).astype(jnp.int32)
    coil_amps = place_ends(jax.random.randint(key_of[2], (COEFS,), -4, 5), jax.random.fold_in(key_of[2], 1), -4, 4).astype(jnp.int32)
    nu_low = jnp.clip(jax.random.uniform(key_of[3], (3,), jnp.float32, 0.2, 1.0), 0.2, 1.0)
    nu_rise = jnp.clip(jax.random.uniform(key_of[4], (3,), jnp.float32, 0.5, 2.0), 0.5, 2.0)
    conductivity = jnp.clip(jnp.exp(jax.random.uniform(key_of[5], (3,), jnp.float32, math.log(0.5), math.log(4.0))), 0.5, 4.0)
    return dict(potential_start=potential_start, material=material, coil_amps=coil_amps, nu_low=nu_low, nu_rise=nu_rise, conductivity=conductivity)


relax_factor = 0.5
omega_base = 0.25
saturation = 3.0
coil_scale = 0.5

def basis_table(first, count, samples):
    coef_index = first + jnp.arange(count, dtype=jnp.int32)
    harmonic = 2 * (coef_index // 2) + 1
    sample_index = jnp.arange(samples, dtype=jnp.int32)
    turns = harmonic[:, None] * sample_index[None, :] % samples
    angle_grid = turns.astype(jnp.float32) * (2.0 * math.pi / samples)
    return jnp.where((coef_index % 2 == 0)[:, None], jnp.cos(angle_grid), jnp.sin(angle_grid))

def frequencies(first, count):
    coef_index = first + jnp.arange(count, dtype=jnp.int32)
    return omega_base * (2 * (coef_index // 2) + 1).astype(jnp.float32)

def lookup(values, material):
    return jnp.where(material == 0, values[0], jnp.where(material == 1, values[1], values[2]))

def reluctivity(field_x, field_y, low_cell, rise_cell):
    scaled = jnp.sqrt(1.0 + (field_x * field_x + field_y * field_y) / (saturation * saturation))
    langevin = 1.0 / jnp.tanh(scaled) - 1.0 / scaled
    return low_cell + rise_cell * (1.0 - 3.0 * langevin / scaled)

def time_rate(potential, frequency):
    shape = potential.shape
    paired = potential.reshape((shape[0] // 2, 2) + shape[1:])
    turned = jnp.stack([paired[:, 1], -paired[:, 0]], axis=1).reshape(shape)
    return turned * frequency.reshape((shape[0],) + (1,) * (len(shape) - 1))

def solve_layer(inputs, coil_amps, nu_low, nu_rise, conductivity):
    potential, material = inputs
    basis = basis_table(0, COEFS, NT)
    frequency = frequencies(0, COEFS)
    low_cell = lookup(nu_low, material)
    rise_cell = lookup(nu_rise, material)
    sigma_cell = lookup(conductivity, material)
    source = coil_amps.astype(jnp.float32)[:, None, None] * jnp.where(material == 1, coil_scale, 0.0)[None]
    precond = 4.0 * (low_cell + rise_cell)[None] + sigma_cell[None] * frequency[:, None, None]
    high = lax.Precision.HIGHEST
    for sweep in range(ITERS):
        padded = jnp.pad(potential, ((0, 0), (0, 1), (0, 1)))
        field_x = padded[:, :-1, 1:] - potential
        field_y = potential - padded[:, 1:, :-1]
        sample_x = jnp.einsum('ct,cxy->txy', basis, field_x, precision=high)
        sample_y = jnp.einsum('ct,cxy->txy', basis, field_y, precision=high)
        recip = reluctivity(sample_x, sample_y, low_cell[None], rise_cell[None])
        inten_x = 2.0 / NT * jnp.einsum('ct,txy->cxy', basis, recip * sample_x, precision=high)
        inten_y = 2.0 / NT * jnp.einsum('ct,txy->cxy', basis, recip * sample_y, precision=high)
        behind_x = jnp.pad(inten_y, ((0, 0), (1, 0), (0, 0)))[:, :-1, :]
        behind_y = jnp.pad(inten_x, ((0, 0), (0, 0), (1, 0)))[:, :, :-1]
        curl_h = inten_y - behind_x - (inten_x - behind_y)
        residual = curl_h + sigma_cell[None] * time_rate(potential, frequency) - source
        potential = potential - relax_factor * residual / precond
    current = jnp.einsum('ct,cxy->txy', basis, time_rate(potential, frequency), precision=high)
    heat_layer = sigma_cell * lax.optimization_barrier(jnp.mean(current * current, axis=0)) / COEFS
    return (potential, heat_layer)

def reference(potential_start, material, coil_amps, nu_low, nu_rise, conductivity):
    layered = jnp.transpose(potential_start, (1, 0, 2, 3))
    solved, heat_density = lax.map(lambda pair: solve_layer(pair, coil_amps, nu_low, nu_rise, conductivity), (layered, material))
    return (jnp.transpose(solved, (1, 0, 2, 3)), heat_density)
```

```python
import functools
import math

import jax
import jax.numpy as jnp
from jax import lax
from jax.experimental import pallas as pl
from jax.experimental.pallas import tpu as pltpu
from jax.sharding import PartitionSpec as P


NT = 128
ITERS = 3
HALF = NT // 2
LANES = 128
RIM = 4
STEP = 2

relax_factor = 0.5
omega_base = 0.25
saturation = 3.0
coil_scale = 0.5


def lookup(values, material):
    return jnp.where(material == 0, values[0], jnp.where(material == 1, values[1], values[2]))


def split(value):
    high = value.astype(jnp.bfloat16)
    low = (value - high.astype(jnp.float32)).astype(jnp.bfloat16)
    return high, low


def split_table(value):
    high = lax.reduce_precision(value, 8, 7)
    return high.astype(jnp.bfloat16), (value - high).astype(jnp.bfloat16)


def shifted(value, axis, by):
    length = lax.axis_size(axis)
    return lax.ppermute(value, axis, [(i, i + by) for i in range(length) if 0 <= i + by < length])


def turned(value, by):
    length = lax.axis_size("harm")
    return lax.ppermute(value, "harm", [(i, (i + by) % length) for i in range(length)])


def turned_and_shifted(value, turn, by):
    groups, length = lax.axis_size("harm"), lax.axis_size("sx")
    pairs = []
    for g in range(groups):
        for i in range(length):
            if 0 <= i + by < length:
                pairs.append((g * length + i, (g + turn) % groups * length + i + by))
    return lax.ppermute(value, ("harm", "sx"), pairs)


def gather_kernel(groups, own, layers, parts, rows, columns, place_ref, *refs):
    mains, tops, bottoms = refs[:groups], refs[groups : 2 * groups], refs[2 * groups : 3 * groups]
    image_ref, left_ref, right_ref, stage_ref = refs[3 * groups :]
    span = rows // parts
    for at in range(-RIM, span + RIM):
        pieces = []
        for g in range(groups):
            for layer in range(layers):
                for part in range(parts):
                    x = span * part + at
                    if x < 0:
                        pieces.append(tops[g][:, layer, RIM + x, :])
                    elif x >= rows:
                        pieces.append(bottoms[g][:, layer, x - rows, :])
                    else:
                        pieces.append(mains[g][:, layer, x, :])
        if own % 8 == 0:
            stacked = jnp.concatenate(pieces, axis=0)
        else:
            for k, piece in enumerate(pieces):
                stage_ref[k * own : (k + 1) * own, :] = piece
            stacked = stage_ref[...]
        flipped = jnp.transpose(stacked)
        image_ref[at + RIM] = flipped
        left_ref[at + RIM] = flipped[:8]
        right_ref[at + RIM] = flipped[columns - 8 :]


def solve_kernel(
    groups, own, layers, parts, rows, columns,
    image_ref, ahead_ref, behind_ref, code_ref, table_ref, fwd_ref, inv_ref, weight_ref, heat_scale_ref,
    *refs,
):
    outs, heat_ref = refs[:groups], refs[groups]
    pot, nu_all, nu_sat, gain, turn_gain, feed, samples_0, samples_1, products_0, products_1, last_row, back_x = refs[groups + 1 :]
    samples, products = (samples_0, samples_1), (products_0, products_1)
    span = rows // parts
    total = span + 2 * RIM
    wide = columns + 8

    def load(x, carry):
        code = code_ref[x]
        chosen = jnp.concatenate([jnp.where(code == m, 1.0, 0.0) for m in (1.0, 2.0, 3.0)] * 3, axis=0)
        picked = lax.dot_general(
            chosen.astype(jnp.bfloat16), table_ref[...], (((0,), (0,)), ((), ())), preferred_element_type=jnp.float32)
        for k, ref in enumerate((nu_all, nu_sat, gain, turn_gain, feed)):
            ref[x] = picked[:wide, k * LANES : (k + 1) * LANES]
        pot[x, 0:columns, :] = image_ref[x]
        edge = lax.broadcasted_iota(jnp.int32, (8, LANES), 0) < RIM
        pot[x, columns:wide, :] = jnp.where(edge, ahead_ref[x], behind_ref[x])
        pot[x, wide : wide + 8, :] = image_ref[x, 0:8, :]
        return carry

    lax.fori_loop(0, total, load, 0, unroll=4)
    for k in range(4 * STEP):
        pot[total + k] = jnp.zeros((wide + 8, LANES), jnp.float32)
    even = lax.broadcasted_iota(jnp.int32, (wide, LANES), 1) % 2 == 0

    def fields_at(base):
        here = [pot[base + k, 0:wide, :] for k in range(STEP + 1)]
        field_x = [pot[base + k, 1 : wide + 1, :] - here[k] for k in range(STEP)]
        field_y = [here[k] - here[k + 1] for k in range(STEP)]
        return here, field_x, field_y

    def to_samples(base, slot):
        _, field_x, field_y = fields_at(base)
        fields = jnp.concatenate([f for pair in zip(field_x, field_y) for f in pair], axis=0)
        high, low = split(fields)
        samples[slot][...] = jnp.dot(
            jnp.concatenate([high, low, high], axis=1), fwd_ref[...], preferred_element_type=jnp.float32)

    def saturate(slot):
        for k in range(STEP):
            sample_x = samples[slot][2 * k * wide : (2 * k + 1) * wide, :]
            sample_y = samples[slot][(2 * k + 1) * wide : (2 * k + 2) * wide, :]
            square = 1.0 + (sample_x * sample_x + sample_y * sample_y)
            scaled = square * lax.rsqrt(square)
            slope = jnp.tanh(scaled)
            factor = (scaled - slope) / (square * slope)
            high, low = split(jnp.concatenate([factor * sample_x, factor * sample_y], axis=0))
            products[slot][2 * k * wide : (2 * k + 2) * wide, 0 : 2 * LANES] = high
            products[slot][2 * k * wide : (2 * k + 2) * wide, 2 * LANES :] = low

    def update(base, slot):
        here, field_x, field_y = fields_at(base)
        pair = jnp.dot(products[slot][...], inv_ref[...], preferred_element_type=jnp.float32)
        back = pair[:, :LANES] + pair[:, LANES:]
        above = last_row[...]
        for k in range(STEP):
            at = base + k
            linear, bent = nu_all[at], nu_sat[at]
            inten_x = linear * field_x[k] - bent * back[2 * k * wide : (2 * k + 1) * wide]
            inten_y = linear * field_y[k] - bent * back[(2 * k + 1) * wide : (2 * k + 2) * wide]
            back_x[k, 8 : wide + 8, :] = inten_x
            back_x[k, 0:8, :] = inten_x[columns:]
            curl = (inten_y - above) - (inten_x - back_x[k, 7 : wide + 7, :])
            above = inten_y
            rotated = jnp.where(even, pltpu.roll(here[k], LANES - 1, 1), pltpu.roll(here[k], 1, 1))
            fresh = here[k] + feed[at] - gain[at] * curl - turn_gain[at] * rotated
            pot[at, 0:wide, :] = fresh
            pot[at, wide : wide + 8, :] = fresh[0:8]
        last_row[...] = above

    def sweep(index, carry):
        first = jnp.where(index == 0, 0, STEP)
        last = jnp.where(index == ITERS - 1, total - 2 * STEP, total - STEP)
        last_row[...] = jnp.zeros((wide, LANES), jnp.float32)
        to_samples(first, 0)
        saturate(0)
        to_samples(first + STEP, 1)

        def advance(step, carry):
            base = first + step * 2 * STEP
            for slot in range(2):
                saturate(1 - slot)
                update(base + slot * STEP, slot)
                to_samples(base + (slot + 2) * STEP, slot)
            return carry

        return lax.fori_loop(0, pl.cdiv(last - first, 2 * STEP), advance, carry)

    lax.fori_loop(0, ITERS, sweep, 0)

    lanes_each = layers * parts * own
    weight = weight_ref[...]

    def finish(block, carry):
        for k in range(8):
            at = pl.multiple_of(block * 8, 8) + k
            flipped = jnp.transpose(pot[block * 8 + k + RIM, 0:columns, :])
            powers = flipped * flipped * weight
            for layer in range(layers):
                for part in range(parts):
                    where = part * span + at
                    power = jnp.zeros((1, columns), jnp.float32)
                    for g in range(groups):
                        begin = g * lanes_each + (layer * parts + part) * own
                        outs[g][:, layer, pl.ds(where, 1), :] = flipped[begin : begin + own].reshape(own, 1, columns)
                        power = power + jnp.sum(powers[begin : begin + own], axis=0, keepdims=True)
                    heat_ref[layer, pl.ds(where, 1), :] = power * heat_scale_ref[layer, pl.ds(where, 1), :]
        return carry

    lax.fori_loop(0, span // 8, finish, 0)


def local(potential_start, material, coil_amps, nu_low, nu_rise, conductivity):
    groups = lax.axis_size("harm")
    place = lax.axis_index("harm")
    own, depth, rows, columns = potential_start.shape
    coefs = own * groups
    slab = depth // groups
    layers = max(d for d in (1, 2) if slab % d == 0)
    parts = LANES // (coefs * layers)
    chunks = slab // layers
    span = rows // parts
    total = span + 2 * RIM
    wide = columns + 8
    cells = layers * parts

    lane = jnp.arange(LANES, dtype=jnp.int32)
    lane_group = lane // (cells * own)
    lane_cell = lane // own % cells
    coef = (place + lane_group) % groups * own + lane % own
    harmonic = 2 * (coef // 2) + 1
    omega = omega_base * harmonic.astype(jnp.float32)
    sign = jnp.where(coef % 2 == 0, 1.0, -1.0)
    slot = jnp.arange(cells * HALF, dtype=jnp.int32)
    turns = harmonic[:, None] * (slot % HALF)[None, :] % NT
    angle = turns.astype(jnp.float32) * (2.0 * math.pi / NT)
    wave = jnp.where((coef % 2 == 0)[:, None], jnp.cos(angle), jnp.sin(angle))
    basis = jnp.where(lane_cell[:, None] == (slot // HALF)[None, :], wave, 0.0)
    fwd_high, fwd_low = split_table(basis / saturation)
    fwd = jnp.concatenate([fwd_high, fwd_high, fwd_low], axis=0)
    inv_high, inv_low = split_table((3.0 * saturation * 2.0 / HALF) * basis.T)
    inv = jnp.concatenate(
        [jnp.concatenate([inv_high, inv_low], axis=1), jnp.concatenate([inv_high, jnp.zeros_like(inv_low)], axis=1)], axis=0)
    amps = coil_amps.astype(jnp.float32)
    amps = jnp.stack([amps] + [turned(amps, -g) for g in range(1, groups)])[lane_group, lane % own]
    precond = 4.0 * (nu_low + nu_rise)[:, None] + conductivity[:, None] * omega[None, :]
    gain = relax_factor / precond
    turn_gain = gain * (conductivity[:, None] * (omega * sign)[None, :])
    feed = gain * jnp.where(jnp.arange(3) == 1, coil_scale, 0.0)[:, None] * amps[None, :]
    constants = jnp.stack(
        [jnp.broadcast_to((nu_low + nu_rise)[:, None], (3, LANES)), jnp.broadcast_to(nu_rise[:, None], (3, LANES)),
         gain, turn_gain, feed], axis=1)
    mine_only = jnp.arange(8)[:, None] == lane_cell[None, :]
    constants = jnp.where(mine_only[None, :, None, :], constants[:, None], 0.0).reshape(24, 5 * LANES)
    top = lax.reduce_precision(constants, 8, 7)
    middle = lax.reduce_precision(constants - top, 8, 7)
    table = jnp.concatenate([top, middle, constants - top - middle], axis=0).astype(jnp.bfloat16)
    weight = jnp.broadcast_to((omega * omega)[:, None], (LANES, columns))

    def part_of(value, group, start, count):
        return lax.dynamic_slice_in_dim(value, group * slab + start, count, 1)

    tops, bottoms = [], []
    arrivals = [[] for _ in range(chunks)]
    for k in range(chunks):
        for g in range(1, groups):
            arrivals[k].append(turned(part_of(potential_start, (place - g) % groups, k * layers, layers), -g))
    for g in range(groups):
        whose = (place - g) % groups
        mine = part_of(potential_start, whose, 0, slab)
        tops.append(turned_and_shifted(mine[:, :, rows - RIM :, :], -g, 1))
        bottoms.append(turned_and_shifted(mine[:, :, :RIM, :], -g, -1))

    slab_material = lax.dynamic_slice_in_dim(material, place * slab, slab, 0)
    heat_scale = lookup(conductivity, slab_material) * (0.5 / coefs)
    code = (slab_material + 1).astype(jnp.float32)
    code = jnp.concatenate(
        [shifted(code[:, rows - RIM :, :], "sx", 1), code, shifted(code[:, :RIM, :], "sx", -1)], axis=1)
    code = jnp.concatenate(
        [code, shifted(code[:, :, :RIM], "sy", -1), shifted(code[:, :, columns - RIM :], "sy", 1)], axis=2)
    code = jnp.stack([code[:, part * span : part * span + total] for part in range(parts)], axis=1)
    code = code.reshape(chunks, cells, total, wide).transpose(0, 2, 1, 3)
    code = jnp.pad(code, ((0, 0), (0, 0), (0, 8 - cells), (0, 0)))

    any_space = pl.BlockSpec(memory_space=pltpu.VMEM)
    gather = pl.pallas_call(
        functools.partial(gather_kernel, groups, own, layers, parts, rows, columns),
        grid_spec=pltpu.PrefetchScalarGridSpec(
            num_scalar_prefetch=1,
            grid=(1,),
            in_specs=[pl.BlockSpec((own, layers, rows, columns), lambda i, s: (0, s[0], 0, 0))]
            + [pl.BlockSpec((own, layers, rows, columns), lambda i, s: (0, 0, 0, 0))] * (groups - 1)
            + [pl.BlockSpec((own, layers, RIM, columns), lambda i, s: (0, s[1], 0, 0))] * (2 * groups),
            out_specs=[
                pl.BlockSpec((total, columns, LANES), lambda i, s: (0, 0, 0)),
                pl.BlockSpec((total, 8, LANES), lambda i, s: (0, 0, 0)),
                pl.BlockSpec((total, 8, LANES), lambda i, s: (0, 0, 0)),
            ],
            scratch_shapes=[pltpu.VMEM((LANES, columns), jnp.float32)],
        ),
        out_shape=[
            jax.ShapeDtypeStruct((total, columns, LANES), jnp.float32),
            jax.ShapeDtypeStruct((total, 8, LANES), jnp.float32),
            jax.ShapeDtypeStruct((total, 8, LANES), jnp.float32),
        ],
        cost_estimate=pl.CostEstimate(flops=0, bytes_accessed=4 * total * columns * LANES * 2, transcendentals=0),
    )
    solve = pl.pallas_call(
        functools.partial(solve_kernel, groups, own, layers, parts, rows, columns),
        in_specs=[any_space] * 9,
        out_specs=[any_space] * (groups + 1),
        out_shape=[jax.ShapeDtypeStruct((own, layers, rows, columns), jnp.float32)] * groups
        + [jax.ShapeDtypeStruct((layers, rows, columns), jnp.float32)],
        scratch_shapes=[pltpu.VMEM((total + 4 * STEP, wide + 8, LANES), jnp.float32)]
        + [pltpu.VMEM((total, wide, LANES), jnp.float32)] * 5
        + [pltpu.VMEM((2 * STEP * wide, 2 * LANES), jnp.float32)] * 2
        + [pltpu.VMEM((2 * STEP * wide, 4 * LANES), jnp.bfloat16)] * 2
        + [pltpu.VMEM((wide, LANES), jnp.float32), pltpu.VMEM((STEP, wide + 8, LANES), jnp.float32)],
        cost_estimate=pl.CostEstimate(
            flops=6 * total * wide * 256 * 256 * 8, bytes_accessed=4 * total * wide * LANES * 4, transcendentals=0),
    )

    potential = jnp.zeros_like(potential_start)
    heats = []
    for k in range(chunks):
        where = jnp.stack([place * chunks + k, jnp.int32(k)]).astype(jnp.int32)
        image, left, right = gather(where, potential_start, *arrivals[k], *tops, *bottoms)
        ahead = shifted(left, "sy", -1)
        behind = shifted(right, "sy", 1)
        *fresh, heat = solve(
            image, ahead, behind, code[k], table, fwd, inv, weight,
            heat_scale[k * layers : (k + 1) * layers])
        heats.append(heat)
        potential = lax.dynamic_update_slice_in_dim(potential, fresh[0], place * slab + k * layers, 1)
        for g in range(1, groups):
            sent = turned(fresh[g], g)
            potential = lax.dynamic_update_slice_in_dim(potential, sent, (place - g) % groups * slab + k * layers, 1)
    return potential, jnp.concatenate(heats, axis=0)


def solution(mesh):
    in_specs = (P("harm", None, "sx", "sy"), P(None, "sx", "sy"), P("harm"), P(), P(), P())
    out_specs = (P("harm", None, "sx", "sy"), P("harm", "sx", "sy"))

    return jax.shard_map(local, mesh=mesh, in_specs=in_specs, out_specs=out_specs, check_vma=False)
```

```python
import functools
import math

import jax
import jax.numpy as jnp
import numpy as np
from jax import lax
from jax.experimental import pallas as pl
from jax.experimental.pallas import tpu as pltpu
from jax.sharding import PartitionSpec as P


NT = 128
ITERS = 3
HALF = NT // 2
LANES = 128
RIM = 4
STEP = 1
UNROLL = 12
SPARE = UNROLL + 4

relax_factor = 0.5
omega_base = 0.25
saturation = 3.0
coil_scale = 0.5


def lookup(values, material):
    return jnp.where(material == 0, values[0], jnp.where(material == 1, values[1], values[2]))


def split(value):
    high = value.astype(jnp.bfloat16)
    low = (value - high.astype(jnp.float32)).astype(jnp.bfloat16)
    return high, low


def shifted(value, axis, by):
    length = lax.axis_size(axis)
    return lax.ppermute(value, axis, [(i, i + by) for i in range(length) if 0 <= i + by < length])


def turned(value, by):
    length = lax.axis_size("harm")
    return lax.ppermute(value, "harm", [(i, (i + by) % length) for i in range(length)])


def turned_and_shifted(value, turn, by):
    groups, length = lax.axis_size("harm"), lax.axis_size("sx")
    pairs = []
    for g in range(groups):
        for i in range(length):
            if 0 <= i + by < length:
                pairs.append((g * length + i, (g + turn) % groups * length + i + by))
    return lax.ppermute(value, ("harm", "sx"), pairs)


def gather_kernel(groups, own, layers, parts, rows, columns, place_ref, *refs):
    mains, tops, bottoms = refs[:groups], refs[groups : 2 * groups], refs[2 * groups : 3 * groups]
    image_ref, left_ref, right_ref, stage_ref = refs[3 * groups :]
    span = rows // parts
    for at in range(-RIM, span + RIM):
        pieces = []
        for g in range(groups):
            for layer in range(layers):
                for part in range(parts):
                    x = span * part + at
                    if x < 0:
                        pieces.append(tops[g][0:own, layer, RIM + x, :])
                    elif x >= rows:
                        pieces.append(bottoms[g][0:own, layer, x - rows, :])
                    else:
                        pieces.append(mains[g][:, layer, x, :])
        if own % 8 == 0:
            stacked = jnp.concatenate(pieces, axis=0)
        else:
            for k, piece in enumerate(pieces):
                stage_ref[k * own : (k + 1) * own, :] = piece
            stacked = stage_ref[...]
        flipped = jnp.transpose(stacked)
        image_ref[0, at + RIM] = flipped
        left_ref[0, at + RIM] = flipped[:8]
        right_ref[0, at + RIM] = flipped[columns - 8 :]


def solve_kernel(
    groups, own, layers, parts, rows, columns,
    chained, place_ref, image_ref, ahead_ref, behind_ref, code_ref, table_ref, fwd_ref, inv_ref, weight_ref, heat_scale_ref,
    *refs,
):
    refs = refs[chained:]
    outs, heat_ref = refs[:groups], refs[groups]
    pot, nu_all, nu_sat, gain, turn_gain, feed, samples_0, samples_1, products_0, products_1, last_row, back_x = refs[groups + 1 :]
    samples, products = (samples_0, samples_1), (products_0, products_1)
    span = rows // parts
    total = span + 2 * RIM
    wide = columns + 8

    def load(x, carry):
        code = code_ref[0, x]
        chosen = jnp.concatenate([jnp.where(code == m, 1.0, 0.0) for m in (1.0, 2.0, 3.0)] * 3, axis=0)
        picked = lax.dot_general(
            chosen.astype(jnp.bfloat16), table_ref[...], (((0,), (0,)), ((), ())), preferred_element_type=jnp.float32)
        for k, ref in enumerate((nu_all, nu_sat, gain, turn_gain, feed)):
            ref[x] = picked[:wide, k * LANES : (k + 1) * LANES]
        pot[x, 0:columns, :] = image_ref[0, x]
        edge = lax.broadcasted_iota(jnp.int32, (8, LANES), 0) < RIM
        pot[x, columns:wide, :] = jnp.where(edge, ahead_ref[0, x], behind_ref[0, x])
        pot[x, wide : wide + 8, :] = image_ref[0, x, 0:8, :]
        return carry

    lax.fori_loop(0, total, load, 0, unroll=4)
    for k in range(SPARE):
        pot[total + k] = jnp.zeros((wide + 8, LANES), jnp.float32)
    even = lax.broadcasted_iota(jnp.int32, (wide, LANES), 1) % 2 == 0

    def fields_at(base):
        here = [pot[base + k, 0:wide, :] for k in range(STEP + 1)]
        field_x = [pot[base + k, 1 : wide + 1, :] - here[k] for k in range(STEP)]
        field_y = [here[k] - here[k + 1] for k in range(STEP)]
        return here, field_x, field_y

    def to_samples(base, slot):
        _, field_x, field_y = fields_at(base)
        fields = jnp.concatenate([f for pair in zip(field_x, field_y) for f in pair], axis=0)
        high, low = split(fields)
        samples[slot][...] = jnp.dot(
            jnp.concatenate([high, low, high], axis=1), fwd_ref[0], preferred_element_type=jnp.float32)

    def saturate(slot):
        for k in range(STEP):
            sample_x = samples[slot][2 * k * wide : (2 * k + 1) * wide, :]
            sample_y = samples[slot][(2 * k + 1) * wide : (2 * k + 2) * wide, :]
            square = 1.0 + (sample_x * sample_x + sample_y * sample_y)
            inverse = lax.rsqrt(square)
            scaled = square * inverse
            factor = inverse * (1.0 / jnp.tanh(scaled) - inverse)
            high, low = split(jnp.concatenate([factor * sample_x, factor * sample_y], axis=0))
            products[slot][2 * k * wide : (2 * k + 2) * wide, 0 : 2 * LANES] = high
            products[slot][2 * k * wide : (2 * k + 2) * wide, 2 * LANES :] = low

    def update(base, slot):
        here, field_x, field_y = fields_at(base)
        pair = jnp.dot(products[slot][...], inv_ref[0], preferred_element_type=jnp.float32)
        back = pair[:, :LANES] + pair[:, LANES:]
        above = last_row[...]
        for k in range(STEP):
            at = base + k
            linear, bent = nu_all[at], nu_sat[at]
            inten_x = linear * field_x[k] - bent * back[2 * k * wide : (2 * k + 1) * wide]
            inten_y = linear * field_y[k] - bent * back[(2 * k + 1) * wide : (2 * k + 2) * wide]
            back_x[k, 8 : wide + 8, :] = inten_x
            back_x[k, 0:8, :] = inten_x[columns:]
            curl = (inten_y - above) - (inten_x - back_x[k, 7 : wide + 7, :])
            above = inten_y
            rotated = jnp.where(even, pltpu.roll(here[k], LANES - 1, 1), pltpu.roll(here[k], 1, 1))
            fresh = here[k] + feed[at] - gain[at] * curl - turn_gain[at] * rotated
            pot[at, 0:wide, :] = fresh
            pot[at, wide : wide + 8, :] = fresh[0:8]
        last_row[...] = above

    def sweep(index, carry):
        first = index + 2
        last = total - 2 - index
        to_samples(first - 1, 1)
        saturate(1)
        to_samples(first, 0)
        pair = jnp.dot(products[1][wide:], inv_ref[0], preferred_element_type=jnp.float32)
        fall = pot[first - 1, 0:wide, :] - pot[first, 0:wide, :]
        last_row[...] = nu_all[first - 1] * fall - nu_sat[first - 1] * (pair[:, :LANES] + pair[:, LANES:])
        saturate(0)
        to_samples(first + STEP, 1)

        def advance(step, carry):
            base = first + step * UNROLL * STEP
            for part in range(UNROLL):
                slot = part % 2
                saturate(1 - slot)
                update(base + part * STEP, slot)
                to_samples(base + (part + 2) * STEP, slot)
            return carry

        return lax.fori_loop(0, pl.cdiv(last - first, UNROLL * STEP), advance, carry)

    lax.fori_loop(0, ITERS, sweep, 0)

    lanes_each = layers * parts * own
    weight = weight_ref[0]

    def finish(block, carry):
        for k in range(8):
            at = pl.multiple_of(block * 8, 8) + k
            flipped = jnp.transpose(pot[block * 8 + k + RIM, 0:columns, :])
            powers = flipped * flipped * weight
            for layer in range(layers):
                for part in range(parts):
                    where = part * span + at
                    power = jnp.zeros((1, columns), jnp.float32)
                    for g in range(groups):
                        begin = g * lanes_each + (layer * parts + part) * own
                        outs[g][:, layer, pl.ds(where, 1), :] = flipped[begin : begin + own].reshape(own, 1, columns)
                        power = power + jnp.sum(powers[begin : begin + own], axis=0, keepdims=True)
                    heat_ref[layer, pl.ds(where, 1), :] = power * heat_scale_ref[layer, pl.ds(where, 1), :]
        return carry

    lax.fori_loop(0, span // 8, finish, 0)


def place_kernel(where_ref, value_ref, whole_ref, out_ref):
    out_ref[...] = value_ref[...]


def lane_tables(groups, own, cells):
    lane = np.arange(LANES)
    cell = lane // own % cells
    slot = np.arange(cells * HALF)
    tables = []
    for place in range(groups):
        coef = (place + lane // (cells * own)) % groups * own + lane % own
        harmonic = 2 * (coef // 2) + 1
        angle = harmonic[:, None] * (slot % HALF)[None, :] % NT * (2.0 * math.pi / NT)
        wave = np.where((coef % 2 == 0)[:, None], np.cos(angle), np.sin(angle))
        basis = np.where(cell[:, None] == (slot // HALF)[None, :], wave, 0.0)

        def halves(value):
            high = value.astype(jnp.bfloat16)
            return high, (value - high.astype(np.float64)).astype(jnp.bfloat16)

        fwd_high, fwd_low = halves(basis / saturation)
        inv_high, inv_low = halves((3.0 * saturation * 2.0 / HALF) * basis.T)
        omega = omega_base * harmonic
        tables.append((
            np.concatenate([fwd_high, fwd_high, fwd_low], axis=0),
            np.block([[inv_high, inv_low], [inv_high, np.zeros_like(inv_low)]]),
            np.repeat((omega * omega).astype(np.float32)[:, None], LANES, axis=1),
            np.stack([omega, omega * np.where(coef % 2 == 0, 1.0, -1.0)]).astype(np.float32),
        ))
    return [np.stack(each) for each in zip(*tables)]


def local(potential_start, material, coil_amps, nu_low, nu_rise, conductivity):
    groups = lax.axis_size("harm")
    place = lax.axis_index("harm")
    own, depth, rows, columns = potential_start.shape
    coefs = own * groups
    slab = depth // groups
    layers = max(d for d in (1, 2) if slab % d == 0)
    parts = LANES // (coefs * layers)
    chunks = slab // layers
    span = rows // parts
    total = span + 2 * RIM
    wide = columns + 8
    cells = layers * parts

    fwd, inv, weight, omegas = lane_tables(groups, own, cells)
    omegas = lax.dynamic_index_in_dim(jnp.asarray(omegas), place, 0, keepdims=False)
    amps = coil_amps.astype(jnp.float32)
    amps = jnp.stack([amps] + [turned(amps, -g) for g in range(1, groups)])
    amps = jnp.broadcast_to(amps[:, None, :], (groups, cells, own)).reshape(1, LANES)
    precond = 4.0 * (nu_low + nu_rise)[:, None] + conductivity[:, None] * omegas[:1]
    gain = relax_factor / precond
    turn_gain = gain * (conductivity[:, None] * omegas[1:])
    feed = gain * jnp.where(jnp.arange(3) == 1, coil_scale, 0.0)[:, None] * amps
    constants = jnp.stack(
        [jnp.broadcast_to((nu_low + nu_rise)[:, None], (3, LANES)), jnp.broadcast_to(nu_rise[:, None], (3, LANES)),
         gain, turn_gain, feed], axis=1)
    mine_only = jnp.arange(8)[:, None] == (jnp.arange(LANES) // own % cells)[None, :]
    constants = jnp.where(mine_only[None, :, None, :], constants[:, None], 0.0).reshape(24, 5 * LANES)
    top = lax.reduce_precision(constants, 8, 7)
    middle = lax.reduce_precision(constants - top, 8, 7)
    table = jnp.concatenate([top, middle, constants - top - middle], axis=0).astype(jnp.bfloat16)

    def part_of(value, group, start, count):
        return lax.dynamic_slice_in_dim(value, group * slab + start, count, 1)

    slab_material = lax.dynamic_slice_in_dim(material, place * slab, slab, 0)
    heat_scale = lookup(conductivity, slab_material) * (0.5 / coefs)
    code = (slab_material + 1).astype(jnp.float32)
    batches = [b for b in ((0, 1), (1, 1), (2, chunks - 2)) if b[0] < chunks]
    tops, bottoms, arrivals = [], [], []
    for start, count in batches:
        arrivals.append([
            turned(part_of(potential_start, (place - g) % groups, start * layers, count * layers), -g)
            for g in range(1, groups)])
    sides = jnp.concatenate(
        [shifted(code[:, :, :RIM], "sy", -1), shifted(code[:, :, columns - RIM :], "sy", 1)], axis=2)
    riders = jnp.stack([code, jnp.pad(sides, ((0, 0), (0, 0), (0, columns - 2 * RIM)))])
    for g in range(groups):
        mine = part_of(potential_start, (place - g) % groups, 0, slab)
        high, low = mine[:, :, rows - RIM :, :], mine[:, :, :RIM, :]
        if g == 0:
            high = jnp.concatenate([high, riders[:, :, rows - RIM :, :]], axis=0)
            low = jnp.concatenate([low, riders[:, :, :RIM, :]], axis=0)
        tops.append(turned_and_shifted(high, -g, 1))
        bottoms.append(turned_and_shifted(low, -g, -1))

    code = jnp.concatenate([tops[0][own:], riders, bottoms[0][own:]], axis=2)
    code = jnp.concatenate([code[0], code[1, :, :, : 2 * RIM]], axis=2)
    code = jnp.stack([code[:, part * span : part * span + total] for part in range(parts)], axis=1)
    code = code.reshape(chunks, cells, total, wide).transpose(0, 2, 1, 3)
    code = jnp.pad(code, ((0, 0), (0, 0), (0, 8 - cells), (0, 0)))

    index = jnp.stack([place, place * chunks]).astype(jnp.int32)

    def gather(start, count, arrived):
        at = (lambda i, s: (0, i, 0, 0))
        return pl.pallas_call(
            functools.partial(gather_kernel, groups, own, layers, parts, rows, columns),
            grid_spec=pltpu.PrefetchScalarGridSpec(
                num_scalar_prefetch=1,
                grid=(count,),
                in_specs=[pl.BlockSpec((own, layers, rows, columns), lambda i, s: (0, s[1] + start + i, 0, 0))]
                + [pl.BlockSpec((own, layers, rows, columns), at)] * (groups - 1)
                + ([pl.BlockSpec((own + 2, layers, RIM, columns), lambda i, s: (0, start + i, 0, 0))]
                   + [pl.BlockSpec((own, layers, RIM, columns), lambda i, s: (0, start + i, 0, 0))] * (groups - 1)) * 2,
                out_specs=[
                    pl.BlockSpec((1, total, columns, LANES), lambda i, s: (i, 0, 0, 0)),
                    pl.BlockSpec((1, total, 8, LANES), lambda i, s: (i, 0, 0, 0)),
                    pl.BlockSpec((1, total, 8, LANES), lambda i, s: (i, 0, 0, 0)),
                ],
                scratch_shapes=[pltpu.VMEM((LANES, columns), jnp.float32)],
            ),
            out_shape=[
                jax.ShapeDtypeStruct((count, total, columns, LANES), jnp.float32),
                jax.ShapeDtypeStruct((count, total, 8, LANES), jnp.float32),
                jax.ShapeDtypeStruct((count, total, 8, LANES), jnp.float32),
            ],
            cost_estimate=pl.CostEstimate(
                flops=0, bytes_accessed=count * 4 * total * columns * LANES * 2, transcendentals=0),
        )(index, potential_start, *arrived, *tops, *bottoms)

    def solve(k, at, image, ahead, behind, potential):
        chained = potential is not None
        fixed = lambda i, s: (0, 0)
        chosen = lambda i, s: (s[0], 0, 0)
        part = lambda i, s: (at, 0, 0, 0)
        whole = jax.ShapeDtypeStruct(potential_start.shape, jnp.float32)
        return pl.pallas_call(
            functools.partial(solve_kernel, groups, own, layers, parts, rows, columns, int(chained)),
            grid_spec=pltpu.PrefetchScalarGridSpec(
                num_scalar_prefetch=1,
                grid=(1,),
                in_specs=[
                    pl.BlockSpec((1, total, columns, LANES), part),
                    pl.BlockSpec((1, total, 8, LANES), part),
                    pl.BlockSpec((1, total, 8, LANES), part),
                    pl.BlockSpec((1, total, 8, wide), lambda i, s: (k, 0, 0, 0)),
                    pl.BlockSpec((72, 5 * LANES), fixed),
                    pl.BlockSpec((1, 3 * LANES, 2 * LANES), chosen),
                    pl.BlockSpec((1, 4 * LANES, 2 * LANES), chosen),
                    pl.BlockSpec((1, LANES, LANES), chosen),
                    pl.BlockSpec((layers, rows, columns), lambda i, s: (k, 0, 0)),
                ] + [pl.BlockSpec(memory_space=pl.ANY)] * chained,
                out_specs=[pl.BlockSpec((own, layers, rows, columns), lambda i, s: (0, s[1] + k, 0, 0))]
                + [pl.BlockSpec((own, layers, rows, columns), lambda i, s: (0, 0, 0, 0))] * (groups - 1)
                + [pl.BlockSpec((layers, rows, columns), lambda i, s: (0, 0, 0))],
                scratch_shapes=[pltpu.VMEM((total + SPARE, wide + 8, LANES), jnp.float32)]
                + [pltpu.VMEM((total + SPARE, wide, LANES), jnp.float32)] * 5
                + [pltpu.VMEM((2 * STEP * wide, 2 * LANES), jnp.float32)] * 2
                + [pltpu.VMEM((2 * STEP * wide, 4 * LANES), jnp.bfloat16)] * 2
                + [pltpu.VMEM((wide, LANES), jnp.float32), pltpu.VMEM((STEP, wide + 8, LANES), jnp.float32)],
            ),
            out_shape=[whole]
            + [jax.ShapeDtypeStruct((own, layers, rows, columns), jnp.float32)] * (groups - 1)
            + [jax.ShapeDtypeStruct((layers, rows, columns), jnp.float32)],
            input_output_aliases={10: 0} if chained else {},
            cost_estimate=pl.CostEstimate(
                flops=6 * total * wide * 256 * 256 * 8, bytes_accessed=4 * total * wide * LANES * 4, transcendentals=0),
        )(index, image, ahead, behind, code, table, fwd, inv, weight, heat_scale, *([potential] if chained else []))

    def place_into(potential, value, block):
        return pl.pallas_call(
            place_kernel,
            grid_spec=pltpu.PrefetchScalarGridSpec(
                num_scalar_prefetch=1,
                grid=(1,),
                in_specs=[pl.BlockSpec((own, layers, rows, columns), lambda i, s: (0, 0, 0, 0)),
                          pl.BlockSpec(memory_space=pl.ANY)],
                out_specs=pl.BlockSpec((own, layers, rows, columns), lambda i, s: (0, s[0], 0, 0)),
            ),
            out_shape=jax.ShapeDtypeStruct(potential.shape, jnp.float32),
            input_output_aliases={2: 0},
            cost_estimate=pl.CostEstimate(
                flops=0, bytes_accessed=8 * own * layers * rows * columns, transcendentals=0),
        )(block, value, potential)

    ready = []
    for k, (start, count) in enumerate(batches):
        image, left, right = gather(start, count, arrivals[k])
        ahead = shifted(left, "sy", -1)
        behind = shifted(right, "sy", 1)
        ready += [(at, image, ahead, behind) for at in range(count)]
    blocks = [(((place - g) % groups) * chunks).astype(jnp.int32) for g in range(groups)]
    potential, heats, coming = None, [], []
    for k in range(chunks):
        potential, *others, heat = solve(k, *ready[k], potential)
        heats.append(heat)
        for value, block in coming:
            potential = place_into(potential, value, block)
        coming = []
        for g in range(1, groups):
            coming.append((turned(others[g - 1], g), blocks[g].reshape(1) + k))
    for value, block in coming:
        potential = place_into(potential, value, block)
    return potential, jnp.concatenate(heats, axis=0)


def solution(mesh):
    in_specs = (P("harm", None, "sx", "sy"), P(None, "sx", "sy"), P("harm"), P(), P(), P())
    out_specs = (P("harm", None, "sx", "sy"), P("harm", "sx", "sy"))

    return jax.shard_map(local, mesh=mesh, in_specs=in_specs, out_specs=out_specs, check_vma=False)
```

```python
import functools
import math

import jax
import jax.numpy as jnp
import numpy as np
from jax import lax
from jax.experimental import pallas as pl
from jax.experimental.pallas import tpu as pltpu
from jax.sharding import PartitionSpec as P


NT = 128
ITERS = 3
HALF = NT // 2
LANES = 128
RIM = 4
STEP = 1
UNROLL = 12
BLOCK = 4
SPARE = UNROLL + 4

relax_factor = 0.5
omega_base = 0.25
saturation = 3.0
coil_scale = 0.5


def lookup(values, material):
    return jnp.where(material == 0, values[0], jnp.where(material == 1, values[1], values[2]))


def split(value):
    high = value.astype(jnp.bfloat16)
    low = (value - high.astype(jnp.float32)).astype(jnp.bfloat16)
    return high, low


def shifted(value, axis, by):
    length = lax.axis_size(axis)
    return lax.ppermute(value, axis, [(i, i + by) for i in range(length) if 0 <= i + by < length])


def turned(value, by):
    length = lax.axis_size("harm")
    return lax.ppermute(value, "harm", [(i, (i + by) % length) for i in range(length)])


def turned_and_shifted(value, turn, by):
    groups, length = lax.axis_size("harm"), lax.axis_size("sx")
    pairs = []
    for g in range(groups):
        for i in range(length):
            if 0 <= i + by < length:
                pairs.append((g * length + i, (g + turn) % groups * length + i + by))
    return lax.ppermute(value, ("harm", "sx"), pairs)


def gather_kernel(groups, own, layers, parts, rows, columns, place_ref, *refs):
    mains, tops, bottoms = refs[:groups], refs[groups : 2 * groups], refs[2 * groups : 3 * groups]
    image_ref, left_ref, right_ref, stage_ref = refs[3 * groups :]
    span = rows // parts
    for at in range(-RIM, span + RIM):
        pieces = []
        for g in range(groups):
            for layer in range(layers):
                for part in range(parts):
                    x = span * part + at
                    if x < 0:
                        pieces.append(tops[g][0:own, layer, RIM + x, :])
                    elif x >= rows:
                        pieces.append(bottoms[g][0:own, layer, x - rows, :])
                    else:
                        pieces.append(mains[g][:, layer, x, :])
        if own % 8 == 0:
            stacked = jnp.concatenate(pieces, axis=0)
        else:
            for k, piece in enumerate(pieces):
                stage_ref[k * own : (k + 1) * own, :] = piece
            stacked = stage_ref[...]
        flipped = jnp.transpose(stacked)
        image_ref[0, at + RIM] = flipped
        left_ref[0, at + RIM] = flipped[:8]
        right_ref[0, at + RIM] = flipped[columns - 8 :]


def solve_kernel(
    groups, own, layers, parts, rows, columns,
    chained, place_ref, image_ref, ahead_ref, behind_ref, code_ref, table_ref, fwd_ref, inv_ref, weight_ref, material_ref, sigma_ref,
    *refs,
):
    refs = refs[chained:]
    outs, heat_ref = refs[:groups], refs[groups]
    pot, nu_all, nu_sat, gain, turn_gain, feed, samples_0, samples_1, products_0, products_1, last_row, back_x = refs[groups + 1 :]
    samples, products = (samples_0, samples_1), (products_0, products_1)
    span = rows // parts
    total = span + 2 * RIM
    wide = columns + 8

    def load(block, carry):
        code = code_ref[0, block]
        chosen = jnp.concatenate([jnp.where(code == m, 1.0, 0.0) for m in (1.0, 2.0, 3.0)] * 3, axis=0)
        picked = lax.dot_general(
            chosen.astype(jnp.bfloat16), table_ref[...], (((0,), (0,)), ((), ())), preferred_element_type=jnp.float32)
        edge = lax.broadcasted_iota(jnp.int32, (8, LANES), 0) < RIM
        for r in range(BLOCK):
            x = block * BLOCK + r
            for k, ref in enumerate((nu_all, nu_sat, gain, turn_gain, feed)):
                ref[x] = picked[r * wide : (r + 1) * wide, k * LANES : (k + 1) * LANES]
            pot[x, 0:columns, :] = image_ref[0, x]
            pot[x, columns:wide, :] = jnp.where(edge, ahead_ref[0, x], behind_ref[0, x])
            pot[x, wide : wide + 8, :] = image_ref[0, x, 0:8, :]
        return carry

    lax.fori_loop(0, total // BLOCK, load, 0, unroll=2)
    for k in range(SPARE):
        pot[total + k] = jnp.zeros((wide + 8, LANES), jnp.float32)
    tiles = [(8 * t, 16 * t) for t in range(wide // 8)]
    even = lax.broadcasted_iota(jnp.int32, (8, LANES), 1) % 2 == 0

    def fields_at(base, y):
        here = pot[base, y : y + 8, :]
        return here, pot[base, y + 1 : y + 9, :] - here, here - pot[base + 1, y : y + 8, :]

    def to_samples(base, slot):
        operand = []
        for y, _ in tiles:
            _, field_x, field_y = fields_at(base, y)
            high, low = split(jnp.concatenate([field_x, field_y], axis=0))
            operand.append(jnp.concatenate([high, low, high], axis=1))
        samples[slot][...] = jnp.dot(
            jnp.concatenate(operand, axis=0), fwd_ref[0], preferred_element_type=jnp.float32)

    def saturate(slot):
        for _, m in tiles:
            sample_x = samples[slot][m : m + 8, :]
            sample_y = samples[slot][m + 8 : m + 16, :]
            square = 1.0 + (sample_x * sample_x + sample_y * sample_y)
            inverse = lax.rsqrt(square)
            factor = inverse * (1.0 / jnp.tanh(square * inverse) - inverse)
            high, low = split(jnp.concatenate([factor * sample_x, factor * sample_y], axis=0))
            products[slot][m : m + 16, 0 : 2 * LANES] = high
            products[slot][m : m + 16, 2 * LANES :] = low

    def intensity(pair, at, y, m, field_x, field_y):
        back = pair[m : m + 16, :LANES] + pair[m : m + 16, LANES:]
        linear, bent = nu_all[at, y : y + 8, :], nu_sat[at, y : y + 8, :]
        return linear * field_x - bent * back[:8], linear * field_y - bent * back[8:]

    def update(at, slot):
        pair = jnp.dot(products[slot][...], inv_ref[0], preferred_element_type=jnp.float32)
        for y, m in tiles[-1:] + tiles[:-1]:
            here, field_x, field_y = fields_at(at, y)
            inten_x, inten_y = intensity(pair, at, y, m, field_x, field_y)
            back_x[y + 8 : y + 16, :] = inten_x
            if y == columns:
                back_x[0:8, :] = inten_x
                held = here, inten_x, inten_y
                continue
            settle(at, y, here, inten_x, inten_y)
        settle(at, columns, *held)

    def settle(at, y, here, inten_x, inten_y):
        curl = (inten_y - last_row[y : y + 8, :]) - (inten_x - back_x[y + 7 : y + 15, :])
        last_row[y : y + 8, :] = inten_y
        rotated = jnp.where(even, pltpu.roll(here, LANES - 1, 1), pltpu.roll(here, 1, 1))
        fresh = (here + feed[at, y : y + 8, :] - gain[at, y : y + 8, :] * curl
                 - turn_gain[at, y : y + 8, :] * rotated)
        pot[at, y : y + 8, :] = fresh
        if y == 0:
            pot[at, wide : wide + 8, :] = fresh

    def sweep(index, carry):
        first = index + 2
        last = total - 2 - index
        to_samples(first - 1, 1)
        saturate(1)
        to_samples(first, 0)
        pair = jnp.dot(products[1][...], inv_ref[0], preferred_element_type=jnp.float32)
        for y, m in tiles:
            _, field_x, field_y = fields_at(first - 1, y)
            last_row[y : y + 8, :] = intensity(pair, first - 1, y, m, field_x, field_y)[1]
        saturate(0)
        to_samples(first + STEP, 1)

        def advance(step, carry):
            base = first + step * UNROLL * STEP
            for part in range(UNROLL):
                slot = part % 2
                saturate(1 - slot)
                update(base + part * STEP, slot)
                to_samples(base + (part + 2) * STEP, slot)
            return carry

        return lax.fori_loop(0, pl.cdiv(last - first, UNROLL * STEP), advance, carry)

    lax.fori_loop(0, ITERS, sweep, 0)

    lanes_each = layers * parts * own
    weight = weight_ref[0]

    def finish(block, carry):
        for k in range(8):
            at = pl.multiple_of(block * 8, 8) + k
            flipped = jnp.transpose(pot[block * 8 + k + RIM, 0:columns, :])
            powers = flipped * flipped * weight
            for layer in range(layers):
                for part in range(parts):
                    where = part * span + at
                    power = jnp.zeros((1, columns), jnp.float32)
                    for g in range(groups):
                        begin = g * lanes_each + (layer * parts + part) * own
                        outs[g][:, layer, pl.ds(where, 1), :] = flipped[begin : begin + own].reshape(own, 1, columns)
                        power = power + jnp.sum(powers[begin : begin + own], axis=0, keepdims=True)
                    sigma = lookup([sigma_ref[m] for m in range(3)], material_ref[layer, pl.ds(where, 1), :])
                    heat_ref[layer, pl.ds(where, 1), :] = power * sigma * (0.5 / (own * groups))
        return carry

    lax.fori_loop(0, span // 8, finish, 0)


def place_kernel(where_ref, value_ref, whole_ref, out_ref):
    out_ref[...] = value_ref[...]


def lane_tables(groups, own, cells):
    lane = np.arange(LANES)
    cell = lane // own % cells
    slot = np.arange(cells * HALF)
    tables = []
    for place in range(groups):
        coef = (place + lane // (cells * own)) % groups * own + lane % own
        harmonic = 2 * (coef // 2) + 1
        angle = harmonic[:, None] * (slot % HALF)[None, :] % NT * (2.0 * math.pi / NT)
        wave = np.where((coef % 2 == 0)[:, None], np.cos(angle), np.sin(angle))
        basis = np.where(cell[:, None] == (slot // HALF)[None, :], wave, 0.0)

        def halves(value):
            high = value.astype(jnp.bfloat16)
            return high, (value - high.astype(np.float64)).astype(jnp.bfloat16)

        fwd_high, fwd_low = halves(basis / saturation)
        inv_high, inv_low = halves((3.0 * saturation * 2.0 / HALF) * basis.T)
        omega = omega_base * harmonic
        tables.append((
            np.concatenate([fwd_high, fwd_high, fwd_low], axis=0),
            np.block([[inv_high, inv_low], [inv_high, np.zeros_like(inv_low)]]),
            np.repeat((omega * omega).astype(np.float32)[:, None], LANES, axis=1),
            np.stack([omega, omega * np.where(coef % 2 == 0, 1.0, -1.0)]).astype(np.float32),
        ))
    return [np.stack(each) for each in zip(*tables)]


def local(potential_start, material, coil_amps, nu_low, nu_rise, conductivity):
    groups = lax.axis_size("harm")
    place = lax.axis_index("harm")
    own, depth, rows, columns = potential_start.shape
    coefs = own * groups
    slab = depth // groups
    layers = max(d for d in (1, 2) if slab % d == 0)
    parts = LANES // (coefs * layers)
    chunks = slab // layers
    span = rows // parts
    total = span + 2 * RIM
    wide = columns + 8
    cells = layers * parts

    fwd, inv, weight, omegas = lane_tables(groups, own, cells)
    omegas = lax.dynamic_index_in_dim(jnp.asarray(omegas), place, 0, keepdims=False)
    amps = coil_amps.astype(jnp.float32)
    amps = jnp.stack([amps] + [turned(amps, -g) for g in range(1, groups)])
    amps = jnp.broadcast_to(amps[:, None, :], (groups, cells, own)).reshape(1, LANES)
    precond = 4.0 * (nu_low + nu_rise)[:, None] + conductivity[:, None] * omegas[:1]
    gain = relax_factor / precond
    turn_gain = gain * (conductivity[:, None] * omegas[1:])
    feed = gain * jnp.where(jnp.arange(3) == 1, coil_scale, 0.0)[:, None] * amps
    constants = jnp.stack(
        [jnp.broadcast_to((nu_low + nu_rise)[:, None], (3, LANES)), jnp.broadcast_to(nu_rise[:, None], (3, LANES)),
         gain, turn_gain, feed], axis=1)
    mine_only = jnp.arange(8)[:, None] == (jnp.arange(LANES) // own % cells)[None, :]
    constants = jnp.where(mine_only[None, :, None, :], constants[:, None], 0.0).reshape(24, 5 * LANES)
    top = lax.reduce_precision(constants, 8, 7)
    middle = lax.reduce_precision(constants - top, 8, 7)
    table = jnp.concatenate([top, middle, constants - top - middle], axis=0).astype(jnp.bfloat16)

    def part_of(value, group, start, count):
        return lax.dynamic_slice_in_dim(value, group * slab + start, count, 1)

    slab_material = lax.dynamic_slice_in_dim(material, place * slab, slab, 0)
    code = (slab_material + 1).astype(jnp.float32)
    batches = [b for b in ((0, 1), (1, 1), (2, chunks - 2)) if b[0] < chunks]
    tops, bottoms, arrivals = [], [], []
    for start, count in batches:
        arrivals.append([
            turned(part_of(potential_start, (place - g) % groups, start * layers, count * layers), -g)
            for g in range(1, groups)])
    sides = jnp.concatenate(
        [shifted(code[:, :, :RIM], "sy", -1), shifted(code[:, :, columns - RIM :], "sy", 1)], axis=2)
    riders = jnp.stack([code, jnp.pad(sides, ((0, 0), (0, 0), (0, columns - 2 * RIM)))])
    for g in range(groups):
        mine = part_of(potential_start, (place - g) % groups, 0, slab)
        high, low = mine[:, :, rows - RIM :, :], mine[:, :, :RIM, :]
        if g == 0:
            high = jnp.concatenate([high, riders[:, :, rows - RIM :, :]], axis=0)
            low = jnp.concatenate([low, riders[:, :, :RIM, :]], axis=0)
        tops.append(turned_and_shifted(high, -g, 1))
        bottoms.append(turned_and_shifted(low, -g, -1))

    code = jnp.concatenate([tops[0][own:], riders, bottoms[0][own:]], axis=2)
    code = jnp.concatenate([code[0], code[1, :, :, : 2 * RIM]], axis=2)
    code = jnp.stack([code[:, part * span : part * span + total] for part in range(parts)], axis=1)
    code = code.reshape(chunks, cells, total // BLOCK, BLOCK * wide).transpose(0, 2, 1, 3)
    code = jnp.pad(code, ((0, 0), (0, 0), (0, 8 - cells), (0, 0)))
    index = jnp.stack([place, place * chunks]).astype(jnp.int32)

    def gather(start, count, arrived):
        at = (lambda i, s: (0, i, 0, 0))
        return pl.pallas_call(
            functools.partial(gather_kernel, groups, own, layers, parts, rows, columns),
            grid_spec=pltpu.PrefetchScalarGridSpec(
                num_scalar_prefetch=1,
                grid=(count,),
                in_specs=[pl.BlockSpec((own, layers, rows, columns), lambda i, s: (0, s[1] + start + i, 0, 0))]
                + [pl.BlockSpec((own, layers, rows, columns), at)] * (groups - 1)
                + ([pl.BlockSpec((own + 2, layers, RIM, columns), lambda i, s: (0, start + i, 0, 0))]
                   + [pl.BlockSpec((own, layers, RIM, columns), lambda i, s: (0, start + i, 0, 0))] * (groups - 1)) * 2,
                out_specs=[
                    pl.BlockSpec((1, total, columns, LANES), lambda i, s: (i, 0, 0, 0)),
                    pl.BlockSpec((1, total, 8, LANES), lambda i, s: (i, 0, 0, 0)),
                    pl.BlockSpec((1, total, 8, LANES), lambda i, s: (i, 0, 0, 0)),
                ],
                scratch_shapes=[pltpu.VMEM((LANES, columns), jnp.float32)],
            ),
            out_shape=[
                jax.ShapeDtypeStruct((count, total, columns, LANES), jnp.float32),
                jax.ShapeDtypeStruct((count, total, 8, LANES), jnp.float32),
                jax.ShapeDtypeStruct((count, total, 8, LANES), jnp.float32),
            ],
            cost_estimate=pl.CostEstimate(
                flops=0, bytes_accessed=count * 4 * total * columns * LANES * 2, transcendentals=0),
        )(index, potential_start, *arrived, *tops, *bottoms)

    def solve(k, at, image, ahead, behind, potential):
        chained = potential is not None
        fixed = lambda i, s: (0, 0)
        chosen = lambda i, s: (s[0], 0, 0)
        part = lambda i, s: (at, 0, 0, 0)
        whole = jax.ShapeDtypeStruct(potential_start.shape, jnp.float32)
        return pl.pallas_call(
            functools.partial(solve_kernel, groups, own, layers, parts, rows, columns, int(chained)),
            grid_spec=pltpu.PrefetchScalarGridSpec(
                num_scalar_prefetch=1,
                grid=(1,),
                in_specs=[
                    pl.BlockSpec((1, total, columns, LANES), part),
                    pl.BlockSpec((1, total, 8, LANES), part),
                    pl.BlockSpec((1, total, 8, LANES), part),
                    pl.BlockSpec((1, total // BLOCK, 8, BLOCK * wide), lambda i, s: (k, 0, 0, 0)),
                    pl.BlockSpec((72, 5 * LANES), fixed),
                    pl.BlockSpec((1, 3 * LANES, 2 * LANES), chosen),
                    pl.BlockSpec((1, 4 * LANES, 2 * LANES), chosen),
                    pl.BlockSpec((1, LANES, LANES), chosen),
                    pl.BlockSpec((layers, rows, columns), lambda i, s: (s[1] + k, 0, 0)),
                    pl.BlockSpec(memory_space=pltpu.SMEM),
                ] + [pl.BlockSpec(memory_space=pl.ANY)] * chained,
                out_specs=[pl.BlockSpec((own, layers, rows, columns), lambda i, s: (0, s[1] + k, 0, 0))]
                + [pl.BlockSpec((own, layers, rows, columns), lambda i, s: (0, 0, 0, 0))] * (groups - 1)
                + [pl.BlockSpec((layers, rows, columns), lambda i, s: (0, 0, 0))],
                scratch_shapes=[pltpu.VMEM((total + SPARE, wide + 8, LANES), jnp.float32)]
                + [pltpu.VMEM((total + SPARE, wide, LANES), jnp.float32)] * 5
                + [pltpu.VMEM((2 * STEP * wide, 2 * LANES), jnp.float32)] * 2
                + [pltpu.VMEM((2 * STEP * wide, 4 * LANES), jnp.bfloat16)] * 2
                + [pltpu.VMEM((wide, LANES), jnp.float32), pltpu.VMEM((wide + 8, LANES), jnp.float32)],
            ),
            out_shape=[whole]
            + [jax.ShapeDtypeStruct((own, layers, rows, columns), jnp.float32)] * (groups - 1)
            + [jax.ShapeDtypeStruct((layers, rows, columns), jnp.float32)],
            input_output_aliases={11: 0} if chained else {},
            cost_estimate=pl.CostEstimate(
                flops=6 * total * wide * 256 * 256 * 8, bytes_accessed=4 * total * wide * LANES * 4, transcendentals=0),
        )(index, image, ahead, behind, code, table, fwd, inv, weight, material, conductivity, *([potential] if chained else []))

    def place_into(potential, value, block):
        return pl.pallas_call(
            place_kernel,
            grid_spec=pltpu.PrefetchScalarGridSpec(
                num_scalar_prefetch=1,
                grid=(1,),
                in_specs=[pl.BlockSpec((own, layers, rows, columns), lambda i, s: (0, 0, 0, 0)),
                          pl.BlockSpec(memory_space=pl.ANY)],
                out_specs=pl.BlockSpec((own, layers, rows, columns), lambda i, s: (0, s[0], 0, 0)),
            ),
            out_shape=jax.ShapeDtypeStruct(potential.shape, jnp.float32),
            input_output_aliases={2: 0},
            cost_estimate=pl.CostEstimate(
                flops=0, bytes_accessed=8 * own * layers * rows * columns, transcendentals=0),
        )(block, value, potential)

    ready = []
    for k, (start, count) in enumerate(batches):
        image, left, right = gather(start, count, arrivals[k])
        ahead = shifted(left, "sy", -1)
        behind = shifted(right, "sy", 1)
        ready += [(at, image, ahead, behind) for at in range(count)]
    blocks = [(((place - g) % groups) * chunks).astype(jnp.int32) for g in range(groups)]
    potential, heats, coming = None, [], []
    for k in range(chunks):
        potential, *others, heat = solve(k, *ready[k], potential)
        heats.append(heat)
        for g in range(1, groups):
            coming.append((turned(others[g - 1], g), blocks[g].reshape(1) + k))
    for value, block in coming:
        potential = place_into(potential, value, block)
    return potential, jnp.concatenate(heats, axis=0)


def solution(mesh):
    in_specs = (P("harm", None, "sx", "sy"), P(None, "sx", "sy"), P("harm"), P(), P(), P())
    out_specs = (P("harm", None, "sx", "sy"), P("harm", "sx", "sy"))

    return jax.shard_map(local, mesh=mesh, in_specs=in_specs, out_specs=out_specs, check_vma=False)
```

```python
import functools
import math

import jax
import jax.numpy as jnp
import numpy as np
from jax import lax
from jax.experimental import pallas as pl
from jax.experimental.pallas import tpu as pltpu
from jax.sharding import PartitionSpec as P


NT = 128
ITERS = 3
HALF = NT // 2
LANES = 128
RIM = 4
STEP = 1
UNROLL = 12
BLOCK = 4
SPARE = UNROLL + 4

relax_factor = 0.5
omega_base = 0.25
saturation = 3.0
coil_scale = 0.5


def lookup(values, material):
    return jnp.where(material == 0, values[0], jnp.where(material == 1, values[1], values[2]))


def split(value):
    high = value.astype(jnp.bfloat16)
    low = (value - high.astype(jnp.float32)).astype(jnp.bfloat16)
    return high, low


def shifted(value, axis, by):
    length = lax.axis_size(axis)
    return lax.ppermute(value, axis, [(i, i + by) for i in range(length) if 0 <= i + by < length])


def turned(value, by):
    length = lax.axis_size("harm")
    return lax.ppermute(value, "harm", [(i, (i + by) % length) for i in range(length)])


def turned_and_shifted(value, turn, by):
    groups, length = lax.axis_size("harm"), lax.axis_size("sx")
    pairs = []
    for g in range(groups):
        for i in range(length):
            if 0 <= i + by < length:
                pairs.append((g * length + i, (g + turn) % groups * length + i + by))
    return lax.ppermute(value, ("harm", "sx"), pairs)


def gather_kernel(groups, own, layers, parts, rows, columns, place_ref, *refs):
    mains, tops, bottoms = refs[:groups], refs[groups : 2 * groups], refs[2 * groups : 3 * groups]
    image_ref, left_ref, right_ref, stage_ref = refs[3 * groups :]
    span = rows // parts
    for at in range(-RIM, span + RIM):
        pieces = []
        for g in range(groups):
            for layer in range(layers):
                for part in range(parts):
                    x = span * part + at
                    if x < 0:
                        pieces.append(tops[g][0:own, layer, RIM + x, :])
                    elif x >= rows:
                        pieces.append(bottoms[g][0:own, layer, x - rows, :])
                    else:
                        pieces.append(mains[g][:, layer, x, :])
        if own % 8 == 0:
            stacked = jnp.concatenate(pieces, axis=0)
        else:
            for k, piece in enumerate(pieces):
                stage_ref[k * own : (k + 1) * own, :] = piece
            stacked = stage_ref[...]
        flipped = jnp.transpose(stacked)
        image_ref[0, at + RIM] = flipped
        left_ref[0, at + RIM] = flipped[:8]
        right_ref[0, at + RIM] = flipped[columns - 8 :]


def solve_kernel(
    groups, own, layers, parts, rows, columns,
    chained, chunk, place_ref, image_ref, ahead_ref, behind_ref, code_ref, table_ref, fwd_ref, inv_ref, weight_ref, material_ref, sigma_ref,
    *refs,
):
    refs = refs[chained:]
    outs, heat_ref = refs[:groups], refs[groups]
    pot, nu_all, nu_sat, gain, turn_gain, feed, samples_0, samples_1, products_0, products_1, last_row, back_x, arrived = refs[groups + 1 :]
    samples, products = (samples_0, samples_1), (products_0, products_1)
    span = rows // parts
    total = span + 2 * RIM
    wide = columns + 8

    def load(block, carry):
        code = code_ref[0, block]
        chosen = jnp.concatenate([jnp.where(code == m, 1.0, 0.0) for m in (1.0, 2.0, 3.0)] * 3, axis=0)
        picked = lax.dot_general(
            chosen.astype(jnp.bfloat16), table_ref[...], (((0,), (0,)), ((), ())), preferred_element_type=jnp.float32)
        for r in range(BLOCK):
            x = block * BLOCK + r
            for k, ref in enumerate((nu_all, nu_sat, gain, turn_gain, feed)):
                ref[x] = picked[r * wide : (r + 1) * wide, k * LANES : (k + 1) * LANES]
        return carry

    def frame(x, carry):
        edge = lax.broadcasted_iota(jnp.int32, (8, LANES), 0) < RIM
        pot[x, columns:wide, :] = jnp.where(edge, ahead_ref[0, x], behind_ref[0, x])
        pot[x, wide : wide + 8, :] = pot[x, 0:8, :]
        return carry

    fetch = pltpu.make_async_copy(
        image_ref.at[chunk], pot.at[pl.ds(0, total), pl.ds(0, columns), :], arrived)
    fetch.start()

    lax.fori_loop(0, total // BLOCK, load, 0, unroll=2)
    fetch.wait()
    lax.fori_loop(0, total, frame, 0, unroll=8)
    for k in range(SPARE):
        pot[total + k] = jnp.zeros((wide + 8, LANES), jnp.float32)
    tiles = [(8 * t, 16 * t) for t in range(wide // 8)]
    even = lax.broadcasted_iota(jnp.int32, (8, LANES), 1) % 2 == 0

    def fields_at(base, y):
        here = pot[base, y : y + 8, :]
        return here, pot[base, y + 1 : y + 9, :] - here, here - pot[base + 1, y : y + 8, :]

    def to_samples(base, slot):
        operand = []
        for y, _ in tiles:
            _, field_x, field_y = fields_at(base, y)
            high, low = split(jnp.concatenate([field_x, field_y], axis=0))
            operand.append(jnp.concatenate([high, low, high], axis=1))
        samples[slot][...] = jnp.dot(
            jnp.concatenate(operand, axis=0), fwd_ref[0], preferred_element_type=jnp.float32)

    def saturate(slot):
        for _, m in tiles:
            sample_x = samples[slot][m : m + 8, :]
            sample_y = samples[slot][m + 8 : m + 16, :]
            square = 1.0 + (sample_x * sample_x + sample_y * sample_y)
            inverse = lax.rsqrt(square)
            factor = inverse * (1.0 / jnp.tanh(square * inverse) - inverse)
            high, low = split(jnp.concatenate([factor * sample_x, factor * sample_y], axis=0))
            products[slot][m : m + 16, 0 : 2 * LANES] = high
            products[slot][m : m + 16, 2 * LANES :] = low

    def intensity(pair, at, y, m, field_x, field_y):
        back = pair[m : m + 16, :LANES] + pair[m : m + 16, LANES:]
        linear, bent = nu_all[at, y : y + 8, :], nu_sat[at, y : y + 8, :]
        return linear * field_x - bent * back[:8], linear * field_y - bent * back[8:]

    def update(at, slot):
        pair = jnp.dot(products[slot][...], inv_ref[0], preferred_element_type=jnp.float32)
        for y, m in tiles[-1:] + tiles[:-1]:
            here, field_x, field_y = fields_at(at, y)
            inten_x, inten_y = intensity(pair, at, y, m, field_x, field_y)
            back_x[y + 8 : y + 16, :] = inten_x
            if y == columns:
                back_x[0:8, :] = inten_x
                held = here, inten_x, inten_y
                continue
            settle(at, y, here, inten_x, inten_y)
        settle(at, columns, *held)

    def settle(at, y, here, inten_x, inten_y):
        curl = (inten_y - last_row[y : y + 8, :]) - (inten_x - back_x[y + 7 : y + 15, :])
        last_row[y : y + 8, :] = inten_y
        rotated = jnp.where(even, pltpu.roll(here, LANES - 1, 1), pltpu.roll(here, 1, 1))
        fresh = (here + feed[at, y : y + 8, :] - gain[at, y : y + 8, :] * curl
                 - turn_gain[at, y : y + 8, :] * rotated)
        pot[at, y : y + 8, :] = fresh
        if y == 0:
            pot[at, wide : wide + 8, :] = fresh

    def sweep(index, carry):
        first = index + 2
        last = total - 2 - index
        to_samples(first - 1, 1)
        saturate(1)
        to_samples(first, 0)
        pair = jnp.dot(products[1][...], inv_ref[0], preferred_element_type=jnp.float32)
        for y, m in tiles:
            _, field_x, field_y = fields_at(first - 1, y)
            last_row[y : y + 8, :] = intensity(pair, first - 1, y, m, field_x, field_y)[1]
        saturate(0)
        to_samples(first + STEP, 1)

        def advance(step, carry):
            base = first + step * UNROLL * STEP
            for part in range(UNROLL):
                slot = part % 2
                saturate(1 - slot)
                update(base + part * STEP, slot)
                to_samples(base + (part + 2) * STEP, slot)
            return carry

        return lax.fori_loop(0, pl.cdiv(last - first, UNROLL * STEP), advance, carry)

    lax.fori_loop(0, ITERS, sweep, 0)

    lanes_each = layers * parts * own
    weight = weight_ref[0]

    def finish(block, carry):
        for k in range(8):
            at = pl.multiple_of(block * 8, 8) + k
            flipped = jnp.transpose(pot[block * 8 + k + RIM, 0:columns, :])
            powers = flipped * flipped * weight
            for layer in range(layers):
                for part in range(parts):
                    where = part * span + at
                    power = jnp.zeros((1, columns), jnp.float32)
                    for g in range(groups):
                        begin = g * lanes_each + (layer * parts + part) * own
                        outs[g][:, layer, pl.ds(where, 1), :] = flipped[begin : begin + own].reshape(own, 1, columns)
                        power = power + jnp.sum(powers[begin : begin + own], axis=0, keepdims=True)
                    sigma = lookup([sigma_ref[m] for m in range(3)], material_ref[layer, pl.ds(where, 1), :])
                    heat_ref[layer, pl.ds(where, 1), :] = power * sigma * (0.5 / (own * groups))
        return carry

    lax.fori_loop(0, span // 8, finish, 0)


def place_kernel(where_ref, value_ref, whole_ref, out_ref):
    out_ref[...] = value_ref[...]


def lane_tables(groups, own, cells):
    lane = np.arange(LANES)
    cell = lane // own % cells
    slot = np.arange(cells * HALF)
    tables = []
    for place in range(groups):
        coef = (place + lane // (cells * own)) % groups * own + lane % own
        harmonic = 2 * (coef // 2) + 1
        angle = harmonic[:, None] * (slot % HALF)[None, :] % NT * (2.0 * math.pi / NT)
        wave = np.where((coef % 2 == 0)[:, None], np.cos(angle), np.sin(angle))
        basis = np.where(cell[:, None] == (slot // HALF)[None, :], wave, 0.0)

        def halves(value):
            high = value.astype(jnp.bfloat16)
            return high, (value - high.astype(np.float64)).astype(jnp.bfloat16)

        fwd_high, fwd_low = halves(basis / saturation)
        inv_high, inv_low = halves((3.0 * saturation * 2.0 / HALF) * basis.T)
        omega = omega_base * harmonic
        tables.append((
            np.concatenate([fwd_high, fwd_high, fwd_low], axis=0),
            np.block([[inv_high, inv_low], [inv_high, np.zeros_like(inv_low)]]),
            np.repeat((omega * omega).astype(np.float32)[:, None], LANES, axis=1),
            np.stack([omega, omega * np.where(coef % 2 == 0, 1.0, -1.0)]).astype(np.float32),
        ))
    return [np.stack(each) for each in zip(*tables)]


def local(potential_start, material, coil_amps, nu_low, nu_rise, conductivity):
    groups = lax.axis_size("harm")
    place = lax.axis_index("harm")
    own, depth, rows, columns = potential_start.shape
    coefs = own * groups
    slab = depth // groups
    layers = max(d for d in (1, 2) if slab % d == 0)
    parts = LANES // (coefs * layers)
    chunks = slab // layers
    span = rows // parts
    total = span + 2 * RIM
    wide = columns + 8
    cells = layers * parts

    fwd, inv, weight, omegas = lane_tables(groups, own, cells)
    omegas = lax.dynamic_index_in_dim(jnp.asarray(omegas), place, 0, keepdims=False)
    amps = coil_amps.astype(jnp.float32)
    amps = jnp.stack([amps] + [turned(amps, -g) for g in range(1, groups)])
    amps = jnp.broadcast_to(amps[:, None, :], (groups, cells, own)).reshape(1, LANES)
    precond = 4.0 * (nu_low + nu_rise)[:, None] + conductivity[:, None] * omegas[:1]
    gain = relax_factor / precond
    turn_gain = gain * (conductivity[:, None] * omegas[1:])
    feed = gain * jnp.where(jnp.arange(3) == 1, coil_scale, 0.0)[:, None] * amps
    constants = jnp.stack(
        [jnp.broadcast_to((nu_low + nu_rise)[:, None], (3, LANES)), jnp.broadcast_to(nu_rise[:, None], (3, LANES)),
         gain, turn_gain, feed], axis=1)
    mine_only = jnp.arange(8)[:, None] == (jnp.arange(LANES) // own % cells)[None, :]
    constants = jnp.where(mine_only[None, :, None, :], constants[:, None], 0.0).reshape(24, 5 * LANES)
    top = lax.reduce_precision(constants, 8, 7)
    middle = lax.reduce_precision(constants - top, 8, 7)
    table = jnp.concatenate([top, middle, constants - top - middle], axis=0).astype(jnp.bfloat16)

    def part_of(value, group, start, count):
        return lax.dynamic_slice_in_dim(value, group * slab + start, count, 1)

    slab_material = lax.dynamic_slice_in_dim(material, place * slab, slab, 0)
    code = (slab_material + 1).astype(jnp.float32)
    batches = [b for b in ((0, 1), (1, 1), (2, chunks - 2)) if b[0] < chunks]
    tops, bottoms, arrivals = [], [], []
    for start, count in batches:
        arrivals.append([
            turned(part_of(potential_start, (place - g) % groups, start * layers, count * layers), -g)
            for g in range(1, groups)])
    sides = jnp.concatenate(
        [shifted(code[:, :, :RIM], "sy", -1), shifted(code[:, :, columns - RIM :], "sy", 1)], axis=2)
    riders = jnp.stack([code, jnp.pad(sides, ((0, 0), (0, 0), (0, columns - 2 * RIM)))])
    for g in range(groups):
        mine = part_of(potential_start, (place - g) % groups, 0, slab)
        high, low = mine[:, :, rows - RIM :, :], mine[:, :, :RIM, :]
        if g == 0:
            high = jnp.concatenate([high, riders[:, :, rows - RIM :, :]], axis=0)
            low = jnp.concatenate([low, riders[:, :, :RIM, :]], axis=0)
        tops.append(turned_and_shifted(high, -g, 1))
        bottoms.append(turned_and_shifted(low, -g, -1))

    code = jnp.concatenate([tops[0][own:], riders, bottoms[0][own:]], axis=2)
    code = jnp.concatenate([code[0], code[1, :, :, : 2 * RIM]], axis=2)
    code = jnp.stack([code[:, part * span : part * span + total] for part in range(parts)], axis=1)
    code = code.reshape(chunks, cells, total // BLOCK, BLOCK * wide).transpose(0, 2, 1, 3)
    code = jnp.pad(code, ((0, 0), (0, 0), (0, 8 - cells), (0, 0)))
    index = jnp.stack([place, place * chunks]).astype(jnp.int32)

    def gather(start, count, arrived):
        at = (lambda i, s: (0, i, 0, 0))
        return pl.pallas_call(
            functools.partial(gather_kernel, groups, own, layers, parts, rows, columns),
            grid_spec=pltpu.PrefetchScalarGridSpec(
                num_scalar_prefetch=1,
                grid=(count,),
                in_specs=[pl.BlockSpec((own, layers, rows, columns), lambda i, s: (0, s[1] + start + i, 0, 0))]
                + [pl.BlockSpec((own, layers, rows, columns), at)] * (groups - 1)
                + ([pl.BlockSpec((own + 2, layers, RIM, columns), lambda i, s: (0, start + i, 0, 0))]
                   + [pl.BlockSpec((own, layers, RIM, columns), lambda i, s: (0, start + i, 0, 0))] * (groups - 1)) * 2,
                out_specs=[
                    pl.BlockSpec((1, total, columns, LANES), lambda i, s: (i, 0, 0, 0)),
                    pl.BlockSpec((1, total, 8, LANES), lambda i, s: (i, 0, 0, 0)),
                    pl.BlockSpec((1, total, 8, LANES), lambda i, s: (i, 0, 0, 0)),
                ],
                scratch_shapes=[pltpu.VMEM((LANES, columns), jnp.float32)],
            ),
            out_shape=[
                jax.ShapeDtypeStruct((count, total, columns, LANES), jnp.float32),
                jax.ShapeDtypeStruct((count, total, 8, LANES), jnp.float32),
                jax.ShapeDtypeStruct((count, total, 8, LANES), jnp.float32),
            ],
            cost_estimate=pl.CostEstimate(
                flops=0, bytes_accessed=count * 4 * total * columns * LANES * 2, transcendentals=0),
        )(index, potential_start, *arrived, *tops, *bottoms)

    def solve(k, at, image, ahead, behind, potential):
        chained = potential is not None
        fixed = lambda i, s: (0, 0)
        chosen = lambda i, s: (s[0], 0, 0)
        part = lambda i, s: (at, 0, 0, 0)
        whole = jax.ShapeDtypeStruct(potential_start.shape, jnp.float32)
        return pl.pallas_call(
            functools.partial(solve_kernel, groups, own, layers, parts, rows, columns, int(chained), at),
            grid_spec=pltpu.PrefetchScalarGridSpec(
                num_scalar_prefetch=1,
                grid=(1,),
                in_specs=[
                    pl.BlockSpec(memory_space=pl.ANY),
                    pl.BlockSpec((1, total, 8, LANES), part),
                    pl.BlockSpec((1, total, 8, LANES), part),
                    pl.BlockSpec((1, total // BLOCK, 8, BLOCK * wide), lambda i, s: (k, 0, 0, 0)),
                    pl.BlockSpec((72, 5 * LANES), fixed),
                    pl.BlockSpec((1, 3 * LANES, 2 * LANES), chosen),
                    pl.BlockSpec((1, 4 * LANES, 2 * LANES), chosen),
                    pl.BlockSpec((1, LANES, LANES), chosen),
                    pl.BlockSpec((layers, rows, columns), lambda i, s: (s[1] + k, 0, 0)),
                    pl.BlockSpec(memory_space=pltpu.SMEM),
                ] + [pl.BlockSpec(memory_space=pl.ANY)] * chained,
                out_specs=[pl.BlockSpec((own, layers, rows, columns), lambda i, s: (0, s[1] + k, 0, 0))]
                + [pl.BlockSpec((own, layers, rows, columns), lambda i, s: (0, 0, 0, 0))] * (groups - 1)
                + [pl.BlockSpec((layers, rows, columns), lambda i, s: (0, 0, 0))],
                scratch_shapes=[pltpu.VMEM((total + SPARE, wide + 8, LANES), jnp.float32)]
                + [pltpu.VMEM((total + SPARE, wide, LANES), jnp.float32)] * 5
                + [pltpu.VMEM((2 * STEP * wide, 2 * LANES), jnp.float32)] * 2
                + [pltpu.VMEM((2 * STEP * wide, 4 * LANES), jnp.bfloat16)] * 2
                + [pltpu.VMEM((wide, LANES), jnp.float32), pltpu.VMEM((wide + 8, LANES), jnp.float32), pltpu.SemaphoreType.DMA(())],
            ),
            out_shape=[whole]
            + [jax.ShapeDtypeStruct((own, layers, rows, columns), jnp.float32)] * (groups - 1)
            + [jax.ShapeDtypeStruct((layers, rows, columns), jnp.float32)],
            input_output_aliases={11: 0} if chained else {},
            cost_estimate=pl.CostEstimate(
                flops=6 * total * wide * 256 * 256 * 8, bytes_accessed=4 * total * wide * LANES * 4, transcendentals=0),
        )(index, image, ahead, behind, code, table, fwd, inv, weight, material, conductivity, *([potential] if chained else []))

    def place_into(potential, value, block):
        return pl.pallas_call(
            place_kernel,
            grid_spec=pltpu.PrefetchScalarGridSpec(
                num_scalar_prefetch=1,
                grid=(1,),
                in_specs=[pl.BlockSpec((own, layers, rows, columns), lambda i, s: (0, 0, 0, 0)),
                          pl.BlockSpec(memory_space=pl.ANY)],
                out_specs=pl.BlockSpec((own, layers, rows, columns), lambda i, s: (0, s[0], 0, 0)),
            ),
            out_shape=jax.ShapeDtypeStruct(potential.shape, jnp.float32),
            input_output_aliases={2: 0},
            cost_estimate=pl.CostEstimate(
                flops=0, bytes_accessed=8 * own * layers * rows * columns, transcendentals=0),
        )(block, value, potential)

    ready = []
    for k, (start, count) in enumerate(batches):
        image, left, right = gather(start, count, arrivals[k])
        ahead = shifted(left, "sy", -1)
        behind = shifted(right, "sy", 1)
        ready += [(at, image, ahead, behind) for at in range(count)]
    blocks = [(((place - g) % groups) * chunks).astype(jnp.int32) for g in range(groups)]
    potential, heats, coming = None, [], []
    for k in range(chunks):
        potential, *others, heat = solve(k, *ready[k], potential)
        heats.append(heat)
        for g in range(1, groups):
            coming.append((turned(others[g - 1], g), blocks[g].reshape(1) + k))
    for value, block in coming:
        potential = place_into(potential, value, block)
    return potential, jnp.concatenate(heats, axis=0)


def solution(mesh):
    in_specs = (P("harm", None, "sx", "sy"), P(None, "sx", "sy"), P("harm"), P(), P(), P())
    out_specs = (P("harm", None, "sx", "sy"), P("harm", "sx", "sy"))

    return jax.shard_map(local, mesh=mesh, in_specs=in_specs, out_specs=out_specs, check_vma=False)
```
